32 devices in a mesh: seq: 8 (over z, y), tp: 4 (over x, core).
Axes of the slice: x: 2, y: 2, z: 4, core: 2. Of those that a mesh axis runs over, the one named last changes fastest.
Arguments:
- tokens: bfloat16 [6144, 2048], P('seq', 'tp'), may hold values from -20 to 20
- w_query: bfloat16 [2048, 2048], P(None, 'tp'), may hold values from -0.125 to 0.125
- w_key: bfloat16 [2048, 2048], P(None, 'tp'), may hold values from -0.125 to 0.125
- w_value: bfloat16 [2048, 2048], P(None, 'tp'), may hold values from -0.125 to 0.125
- head_gain: float32 [2048], P('tp'), may hold values from 0.5 to 1.5
- w_out: bfloat16 [2048, 2048], P('tp'), may hold values from -0.125 to 0.125
- norm_gain: float32 [2048], replicated, may hold values from 0.5 to 1.5
- w_gate: bfloat16 [2048, 8192], P('seq', 'tp'), may hold values from -0.125 to 0.125
- w_up: bfloat16 [2048, 8192], P('seq', 'tp'), may hold values from -0.125 to 0.125
- w_down: bfloat16 [8192, 2048], P('tp', 'seq'), may hold values from -0.0625 to 0.0625
Outputs:
- layer_out: bfloat16 [6144, 2048], P('seq', 'tp')
The draws below stay inside these ranges and needn't reach their ends.
All inputs are finite; a program needn't handle non-finite values.
Results may differ from the reference program's by a relative error of at most 0.009.
Values may be sent and summed in bfloat16 or wider, within the bound.
A program may use at most 128 MiB of HBM per device.

```python
import math
import jax
import jax.numpy as jnp
from jax import lax

D = 2048
HEADS = 16
HD = 128
FF = 8192
L_DEV = 768
TOKENS = 6144
N_SEQ = 8
N_TP = 4


def draw_tokens(key, part):
    key_base = jax.random.fold_in(key, 11)
    key_rows = jax.random.fold_in(key, 12)
    key_columns = jax.random.fold_in(key, 14)
    row_scale = jnp.exp(jax.random.uniform(key_rows, (TOKENS, 1), jnp.float32, math.log(0.5), math.log(5.0)))
    ramp = jnp.arange(D, dtype=jnp.float32)[None, :] / (D - 1.0)
    base = jax.random.normal(key_base, (TOKENS, D), jnp.float32)
    jitter = jax.random.uniform(key_columns, (1, D), jnp.float32, -0.15, 0.15)
    column_scale = jnp.exp(math.log(0.5) + ramp * math.log(4.0) + jitter)
    return jnp.clip(base * column_scale * row_scale, -20.0, 20.0).astype(jnp.bfloat16)


def shard_levels(key, extent, pieces, low, high):
    def one(position, blocks):
        steps = jax.random.uniform(jax.random.fold_in(jax.random.fold_in(key, 6), position), (blocks,), jnp.float32, low / len(pieces), high / len(pieces))
        return jnp.repeat(jnp.exp(steps), extent[position] // blocks).reshape((-1,) + (1,) * (len(extent) - position - 1))

    level = one(*pieces[0])
    for cut in pieces[1:]:
        level = level * one(*cut)
    return level


def centred(own_key, dims, scale, reach, split=(), kind=jnp.bfloat16):
    values = jax.random.normal(own_key, dims, jnp.float32) * scale
    if len(split) > 0:
        values = shard_levels(own_key, dims, split, -0.22, 0.18) * values
    return jnp.clip(values, min=-reach, max=reach).astype(kind)


def setup_inputs(seed: int = 0) -> dict:
    key_of = jax.random.split(jax.random.key(seed), 11)
    return {
        "tokens": draw_tokens(jax.random.fold_in(key_of[10], 71), 0),
        "w_query": centred(key_of[1], (D, D), D ** -0.5, 0.125, ((1, 4),)),
        "w_key": centred(key_of[2], (D, D), D ** -0.5, 0.125, ((1, 4),)),
        "w_value": centred(key_of[3], (D, D), D ** -0.5, 0.125, ((1, 4),)),
        "head_gain": jnp.clip(0.5 + 1.0 * jax.random.uniform(key_of[4], (D,), jnp.float32) ** shard_levels(key_of[4], (D,), ((0, 4),), -0.2, 0.2), 0.5, 1.5),
        "w_out": centred(key_of[5], (D, D), D ** -0.5, 0.125, ((0, 4),)),
        "norm_gain": jnp.clip(jax.random.uniform(key_of[6], (D,), jnp.float32, 0.5, 1.5), 0.5, 1.5),
        "w_gate": centred(key_of[7], (D, FF), D ** -0.5, 0.125, ((0, 8), (1, 4))),
        "w_up": centred(key_of[8], (D, FF), D ** -0.5, 0.125, ((0, 8), (1, 4))),
        "w_down": centred(key_of[9], (FF, D), FF ** -0.5, 0.0625, ((0, 4), (1, 8))),
    }


def reference(tokens, w_query, w_key, w_value, head_gain, w_out, norm_gain, w_gate, w_up, w_down):

    def project(weight):
        return jnp.dot(tokens, weight, preferred_element_type=jnp.float32).astype(jnp.bfloat16)
    query = project(w_query).reshape(N_SEQ, L_DEV, HEADS, HD)
    keys_all = project(w_key).reshape(N_SEQ, L_DEV, HEADS, HD)
    values_all = project(w_value).reshape(N_SEQ, L_DEV, HEADS, HD)
    causal = jnp.arange(L_DEV)[:, None] >= jnp.arange(L_DEV)[None, :]

    def block_step(state, inputs):
        query_block, key_block, value_block = inputs
        qf = query_block.astype(jnp.float32)
        kf = key_block.astype(jnp.float32)
        vf = value_block.astype(jnp.float32)
        scores = jnp.einsum('ihd,jhd->hij', qf, kf)
        scores = jnp.where(causal[None], scores, 0.0).astype(jnp.bfloat16)
        inside = jnp.einsum('hij,jhd->ihd', scores.astype(jnp.float32), vf)
        history = state.astype(jnp.bfloat16).astype(jnp.float32)
        carried = jnp.einsum('ihd,hde->ihe', qf, history)
        new_state = state + jnp.einsum('jhd,jhe->hde', kf, vf)
        return (new_state, inside + carried)
    start_state = jnp.zeros((HEADS, HD, HD), jnp.float32)
    final_state, mixed = lax.scan(block_step, start_state, (query, keys_all, values_all))
    mixed = mixed.reshape(TOKENS, HEADS, HD)
    scale = lax.rsqrt(lax.optimization_barrier(jnp.mean(mixed * mixed, axis=-1, keepdims=True)) + 1e-06)
    normed = (mixed * scale * head_gain.reshape(HEADS, HD)).astype(jnp.bfloat16).reshape(TOKENS, D)
    group_width = D // N_TP
    resid = tokens.astype(jnp.float32)
    for group in range(N_TP):
        lo = group * group_width
        part = jnp.dot(normed[:, lo:lo + group_width], w_out[lo:lo + group_width, :], preferred_element_type=jnp.float32)
        resid = resid + part.astype(jnp.bfloat16).astype(jnp.float32)
    factor = lax.rsqrt(lax.optimization_barrier(jnp.mean(resid * resid, axis=-1, keepdims=True)) + 1e-05)
    ffn_in = (resid * factor * norm_gain).astype(jnp.bfloat16)
    gate = jnp.dot(ffn_in, w_gate, preferred_element_type=jnp.float32)
    upward = jnp.dot(ffn_in, w_up, preferred_element_type=jnp.float32)
    hidden = (jax.nn.silu(gate) * upward).astype(jnp.bfloat16)
    hidden_width = FF // N_TP
    result = resid
    for group in range(N_TP):
        lo = group * hidden_width
        part = jnp.dot(hidden[:, lo:lo + hidden_width], w_down[lo:lo + hidden_width, :], preferred_element_type=jnp.float32)
        result = result + part.astype(jnp.bfloat16).astype(jnp.float32)
    return result.astype(jnp.bfloat16)
```

```python
import jax
import jax.numpy as jnp
from jax import lax
from jax.sharding import PartitionSpec as P

HD = 128
F32 = jnp.float32
BF16 = jnp.bfloat16


def make_body(n_seq, n_tp):
    pair = 2 if n_seq >= 4 else 1
    seq_bits = [1 << b for b in range(n_seq.bit_length() - 1)]
    tp_bits = [1 << b for b in range(n_tp.bit_length() - 1)]
    spread_bits = [b for b in reversed(seq_bits) if b != pair]

    def swap(value, axis, bit):
        size = n_seq if axis == "seq" else n_tp
        return lax.ppermute(value, axis, [(i, i ^ bit) for i in range(size)])

    def spread(held, axis, bits):
        held = dict(held)
        for bit in bits:
            held.update({r ^ bit: swap(v, axis, bit) for r, v in held.items()})
        return held

    def gather_tp(value):
        return spread({0: value}, "tp", list(reversed(tp_bits)))

    def scatter_tp(terms):
        terms = dict(terms)
        for bit in tp_bits:
            for r in [r for r in terms if r & bit]:
                moved = swap(terms.pop(r).astype(BF16), "tp", bit)
                terms[r ^ bit] = terms[r ^ bit] + moved.astype(F32)
        return terms[0]

    def body(tokens, w_query, w_key, w_value, head_gain, w_out, norm_gain, w_gate, w_up, w_down):
        length, width = tokens.shape
        heads = w_query.shape[1] // HD
        model = norm_gain.shape[0]
        me_seq = lax.axis_index("seq")
        me_tp = lax.axis_index("tp")
        part = ((me_seq & pair) != 0).astype(jnp.int32)
        half = w_gate.shape[1] // 2
        rows = w_gate.shape[0]

        def shared(weight, dim):
            keep = lax.dynamic_slice_in_dim(weight, part * half, half, dim)
            give = lax.dynamic_slice_in_dim(weight, (1 - part) * half, half, dim)
            got = swap(give, "seq", pair)
            return spread({0: keep, pair: got}, "seq", spread_bits)

        def assemble(pieces, dim):
            shape = [0, 0]
            shape[dim] = n_seq * rows
            shape[1 - dim] = half
            out = jnp.zeros(shape, BF16)
            for r, piece in pieces.items():
                out = lax.dynamic_update_slice_in_dim(out, piece, (me_seq ^ r) * rows, dim)
            return out

        def matmul(a, b):
            return jnp.dot(a, b, preferred_element_type=F32)

        def over_features(pieces, weight):
            total = None
            for r in sorted(pieces):
                block = lax.dynamic_slice_in_dim(weight, (me_tp ^ r) * width, width, 0)
                term = matmul(pieces[r], block)
                total = term if total is None else total + term
            return total

        def to_features(value, weight):
            terms = {}
            for r in reversed(range(n_tp)):
                block = lax.dynamic_slice_in_dim(weight, (me_tp ^ r) * width, width, 1)
                terms[r] = matmul(value, block)
            return scatter_tp(terms)

        features = gather_tp(tokens)
        gate_pieces = shared(w_gate, 1)
        up_pieces = shared(w_up, 1)
        down_pieces = shared(w_down, 0)

        def project(weight):
            return over_features(features, weight).astype(BF16).reshape(length, heads, HD)

        keys = project(w_key)
        values = project(w_value)
        query = project(w_query)
        state = jnp.einsum("jhd,jhe->hde", keys, values, preferred_element_type=F32)
        history = jnp.zeros_like(state)
        total = state
        for bit in seq_bits:
            other = swap(total, "seq", bit)
            history = history + jnp.where((me_seq & bit) != 0, other, 0.0)
            total = total + other
        scores = jnp.einsum("ihd,jhd->hij", query, keys, preferred_element_type=F32)
        causal = jnp.arange(length)[:, None] >= jnp.arange(length)[None, :]
        scores = jnp.where(causal[None], scores, 0.0).astype(BF16)
        inside = jnp.einsum("hij,jhd->ihd", scores, values, preferred_element_type=F32)
        carried = jnp.einsum(
            "ihd,hde->ihe", query, history.astype(BF16), preferred_element_type=F32
        )
        mixed = inside + carried
        scale = lax.rsqrt(jnp.mean(mixed * mixed, axis=-1, keepdims=True) + 1e-06)
        normed = (mixed * scale * head_gain.reshape(heads, HD)).astype(BF16)
        normed = normed.reshape(length, heads * HD)
        resid = tokens.astype(F32) + to_features(normed, w_out)
        gain = lax.dynamic_slice_in_dim(norm_gain, me_tp * width, width, 0)
        own_in = (resid * gain).astype(BF16)
        pair_in = swap(own_in, "seq", pair)
        own_pieces = gather_tp(own_in)
        pair_pieces = gather_tp(pair_in)
        squares = jnp.sum(resid * resid, axis=-1)
        for bit in tp_bits:
            squares = squares + swap(squares, "tp", bit)
        pair_squares = swap(squares, "seq", pair)
        gate_whole = assemble(gate_pieces, 0)
        up_whole = assemble(up_pieces, 0)
        down_whole = assemble(down_pieces, 1)

        def feed(pieces, total):
            factor = lax.rsqrt(total / model + 1e-05)[:, None]
            gate = over_features(pieces, gate_whole) * factor
            upward = over_features(pieces, up_whole) * factor
            hidden = (jax.nn.silu(gate) * upward).astype(BF16)
            return to_features(hidden, down_whole)

        pair_out = feed(pair_pieces, pair_squares)
        own_out = feed(own_pieces, squares)
        back = swap(pair_out.astype(BF16), "seq", pair)
        return (resid + own_out + back.astype(F32)).astype(BF16)

    return body


def solution(mesh):
    return jax.shard_map(
        make_body(mesh.shape["seq"], mesh.shape["tp"]),
        mesh=mesh,
        in_specs=(
            P("seq", "tp"),
            P(None, "tp"),
            P(None, "tp"),
            P(None, "tp"),
            P("tp"),
            P("tp", None),
            P(),
            P("seq", "tp"),
            P("seq", "tp"),
            P("tp", "seq"),
        ),
        out_specs=P("seq", "tp"),
        check_vma=False,
    )
```

```python
import jax
import jax.numpy as jnp
from jax import lax
from jax.sharding import PartitionSpec as P

HD = 128
F32 = jnp.float32
BF16 = jnp.bfloat16


def make_body(n_seq, n_tp):
    pair = 2 if n_seq >= 4 else 1
    seq_bits = [1 << b for b in range(n_seq.bit_length() - 1)]
    tp_bits = [1 << b for b in range(n_tp.bit_length() - 1)]
    spread_bits = [b for b in reversed(seq_bits) if b != pair]

    def swap(value, axis, bit):
        size = n_seq if axis == "seq" else n_tp
        return lax.ppermute(value, axis, [(i, i ^ bit) for i in range(size)])

    def spread(held, axis, bits):
        held = dict(held)
        for bit in bits:
            held.update({r ^ bit: swap(v, axis, bit) for r, v in held.items()})
        return held

    def gather_tp(value):
        return spread({0: value}, "tp", list(reversed(tp_bits)))

    def scatter_tp(terms):
        terms = dict(terms)
        for bit in tp_bits:
            for r in [r for r in terms if r & bit]:
                moved = swap(terms.pop(r).astype(BF16), "tp", bit)
                terms[r ^ bit] = terms[r ^ bit] + moved.astype(F32)
        return terms[0]

    def body(tokens, w_query, w_key, w_value, head_gain, w_out, norm_gain, w_gate, w_up, w_down):
        length, width = tokens.shape
        heads = w_query.shape[1] // HD
        model = norm_gain.shape[0]
        me_seq = lax.axis_index("seq")
        me_tp = lax.axis_index("tp")
        part = ((me_seq & pair) != 0).astype(jnp.int32)
        half = w_gate.shape[1] // 2
        rows = w_gate.shape[0]

        def halves(weight, dim):
            keep = lax.dynamic_slice_in_dim(weight, part * half, half, dim)
            give = lax.dynamic_slice_in_dim(weight, (1 - part) * half, half, dim)
            return keep, give

        def assemble(pieces, dim):
            shape = list(pieces[0].shape)
            shape[dim] = n_seq * rows
            out = jnp.zeros(shape, BF16)
            for r, piece in pieces.items():
                out = lax.dynamic_update_slice_in_dim(out, piece, (me_seq ^ r) * rows, dim)
            return out

        def after(values, anchor):
            keys_of = list(values)
            out = lax.optimization_barrier(tuple(values[k] for k in keys_of) + (anchor,))
            return dict(zip(keys_of, out[:-1])), out[-1]

        def hops(pieces, bits):
            return {r ^ bit: swap(v, "seq", bit) for bit in bits for r, v in pieces.items()}

        def matmul(a, b):
            return jnp.dot(a, b, preferred_element_type=F32)

        def side_by_side(pieces):
            out = jnp.zeros((length, model), BF16)
            for r in sorted(pieces):
                out = lax.dynamic_update_slice_in_dim(out, pieces[r], (me_tp ^ r) * width, 1)
            return out

        def to_features(value, weight):
            terms = {}
            for r in reversed(range(n_tp)):
                block = lax.dynamic_slice_in_dim(weight, (me_tp ^ r) * width, width, 1)
                terms[r] = matmul(value, block)
            return scatter_tp(terms)

        first, last = spread_bits[:-1], spread_bits[-1:]
        gate_keep, gate_give = halves(w_gate, 1)
        up_keep, up_give = halves(w_up, 1)
        down_keep, down_give = halves(w_down, 0)
        wide_own = {0: jnp.concatenate([gate_keep, up_keep], axis=1)}
        wide_give = jnp.concatenate([gate_give, up_give], axis=1)
        tall_own = {0: down_keep}

        features = side_by_side(gather_tp(tokens))
        wide_far = dict(wide_own)
        for bit in first:
            wide_far.update(hops(wide_far, [bit]))
        wide_got = {pair: swap(wide_give, "seq", pair)}
        tall_got = {pair: swap(down_give, "seq", pair)}

        def project(weight):
            return matmul(features, weight).astype(BF16).reshape(length, heads, HD)

        keys = project(w_key)
        values = project(w_value)
        state = jnp.einsum("jhd,jhe->hde", keys, values, preferred_element_type=F32)
        query = project(w_query)
        history = jnp.zeros_like(state)
        total = state
        for bit in seq_bits:
            other = swap(total.astype(BF16), "seq", bit).astype(F32)
            history = history + jnp.where((me_seq & bit) != 0, other, 0.0)
            total = total + other
        wide_got, query = after(wide_got, query)
        tall_got, query = after(tall_got, query)
        tall_own, query = after(tall_own, query)
        for bit in first:
            wide_got.update(hops(wide_got, [bit]))
        tall = {**tall_own, **tall_got}
        for bit in first:
            tall.update(hops(tall, [bit]))
        wide_near = hops(wide_own, last)
        scores = jnp.einsum("ihd,jhd->hij", query, keys, preferred_element_type=F32)
        causal = jnp.arange(length)[:, None] >= jnp.arange(length)[None, :]
        scores = jnp.where(causal[None], scores, 0.0).astype(BF16)
        inside = jnp.einsum("hij,jhd->ihd", scores, values, preferred_element_type=F32)
        wide = {**wide_far, **wide_got}
        wide.update(wide_near)
        for r in list(wide):
            for bit in last:
                if r ^ bit not in wide:
                    moved, inside = after({r: wide[r]}, inside) if r else ({r: wide[r]}, inside)
                    wide[r] = moved[r]
                    wide[r ^ bit] = swap(moved[r], "seq", bit)
        carried = jnp.einsum(
            "ihd,hde->ihe", query, history.astype(BF16), preferred_element_type=F32
        )
        mixed = inside + carried
        scale = lax.rsqrt(jnp.mean(mixed * mixed, axis=-1, keepdims=True) + 1e-06)
        normed = (mixed * scale * head_gain.reshape(heads, HD)).astype(BF16)
        normed = normed.reshape(length, heads * HD)
        resid = tokens.astype(F32) + to_features(normed, w_out)
        gain = lax.dynamic_slice_in_dim(norm_gain, me_tp * width, width, 0)
        own_in = (resid * gain).astype(BF16)
        tall, own_in = after(tall, own_in)
        for r in list(tall):
            for bit in last:
                tall[r ^ bit] = swap(tall[r], "seq", bit)
        pair_in = swap(own_in, "seq", pair)
        own_pieces = gather_tp(own_in)
        pair_pieces = gather_tp(pair_in)
        squares = jnp.sum(resid * resid, axis=-1)
        for bit in tp_bits:
            squares = squares + swap(squares, "tp", bit)
        pair_squares = swap(squares, "seq", pair)
        wide_whole = assemble(wide, 0)
        gate_whole, up_whole = wide_whole[:, :half], wide_whole[:, half:]
        down_whole = assemble(tall, 1)

        def feed(pieces, total):
            factor = lax.rsqrt(total / model + 1e-05)[:, None]
            ffn_in = side_by_side(pieces)
            gate = matmul(ffn_in, gate_whole) * factor
            upward = matmul(ffn_in, up_whole) * factor
            hidden = (jax.nn.silu(gate) * upward).astype(BF16)
            return to_features(hidden, down_whole)

        pair_out = feed(pair_pieces, pair_squares)
        own_out = feed(own_pieces, squares)
        back = swap(pair_out.astype(BF16), "seq", pair)
        return (resid + own_out + back.astype(F32)).astype(BF16)

    return body


def solution(mesh):
    return jax.shard_map(
        make_body(mesh.shape["seq"], mesh.shape["tp"]),
        mesh=mesh,
        in_specs=(
            P("seq", "tp"),
            P(None, "tp"),
            P(None, "tp"),
            P(None, "tp"),
            P("tp"),
            P("tp", None),
            P(),
            P("seq", "tp"),
            P("seq", "tp"),
            P("tp", "seq"),
        ),
        out_specs=P("seq", "tp"),
        check_vma=False,
    )
```

```python
import jax
import jax.numpy as jnp
from jax import lax
from jax.experimental.layout import Layout, with_layout_constraint
from jax.sharding import PartitionSpec as P

HD = 128
F32 = jnp.float32
BF16 = jnp.bfloat16


def make_body(n_seq, n_tp):
    pair = n_seq // 2
    seq_bits = [1 << b for b in range(n_seq.bit_length() - 1)]
    tp_bits = [1 << b for b in range(n_tp.bit_length() - 1)]
    spread_bits = [b for b in reversed(seq_bits) if b != pair]

    def swap(value, axis, bit):
        size = n_seq if axis == "seq" else n_tp
        return lax.ppermute(value, axis, [(i, i ^ bit) for i in range(size)])

    def spread(held, axis, bits):
        held = dict(held)
        for bit in bits:
            held.update({r ^ bit: swap(v, axis, bit) for r, v in held.items()})
        return held

    def gather_tp(value):
        return spread({0: value}, "tp", list(reversed(tp_bits)))

    def scatter_tp(terms):
        terms = dict(terms)
        for bit in tp_bits:
            for r in [r for r in terms if r & bit]:
                moved = swap(terms.pop(r).astype(BF16), "tp", bit)
                terms[r ^ bit] = terms[r ^ bit] + moved.astype(F32)
        return terms[0]

    def body(tokens, w_query, w_key, w_value, head_gain, w_out, norm_gain, w_gate, w_up, w_down):
        length, width = tokens.shape
        heads = w_query.shape[1] // HD
        model = norm_gain.shape[0]
        me_seq = lax.axis_index("seq")
        me_tp = lax.axis_index("tp")
        part = ((me_seq & pair) != 0).astype(jnp.int32)
        half = w_gate.shape[1] // 2
        rows = w_gate.shape[0]

        def halves(weight, dim):
            keep = lax.dynamic_slice_in_dim(weight, part * half, half, dim)
            give = lax.dynamic_slice_in_dim(weight, (1 - part) * half, half, dim)
            return keep, give

        def assemble(pieces, dim):
            shape = list(pieces[0].shape)
            shape[dim] = n_seq * rows
            out = jnp.zeros(shape, BF16)
            for r, piece in pieces.items():
                out = lax.dynamic_update_slice_in_dim(out, piece, (me_seq ^ r) * rows, dim)
            return out

        def after(values, anchor):
            keys_of = list(values)
            out = lax.optimization_barrier(tuple(values[k] for k in keys_of) + (anchor,))
            return dict(zip(keys_of, out[:-1])), out[-1]

        def hops(pieces, bits):
            return {r ^ bit: swap(v, "seq", bit) for bit in bits for r, v in pieces.items()}

        def matmul(a, b):
            return jnp.dot(a, b, preferred_element_type=F32)

        def side_by_side(pieces):
            out = jnp.zeros((length, model), BF16)
            for r in sorted(pieces):
                out = lax.dynamic_update_slice_in_dim(out, pieces[r], (me_tp ^ r) * width, 1)
            return out

        def to_features(value, weight):
            terms = {}
            for r in reversed(range(n_tp)):
                block = lax.dynamic_slice_in_dim(weight, (me_tp ^ r) * width, width, 1)
                terms[r] = matmul(value, block)
            return scatter_tp(terms)

        first, last = spread_bits[:-1], spread_bits[-1:]
        gate_keep, gate_give = halves(w_gate, 1)
        up_keep, up_give = halves(w_up, 1)
        down_keep, down_give = halves(w_down, 0)
        wide_own = {0: jnp.concatenate([gate_keep, up_keep], axis=1)}
        wide_give = jnp.concatenate([gate_give, up_give], axis=1)
        tall_own = {0: down_keep}

        features = with_layout_constraint(side_by_side(gather_tp(tokens)), Layout((0, 1)))
        wide_got = {pair: swap(wide_give, "seq", pair)}
        wide_far = dict(wide_own)
        for bit in first:
            wide_far.update(hops(wide_far, [bit]))
        wide_near = hops(wide_own, last)
        tall_far = dict(tall_own)
        for bit in first:
            tall_far.update(hops(tall_far, [bit]))
        tall_near = hops(tall_own, last)

        def project(weight):
            return matmul(features, weight).astype(BF16).reshape(length, heads, HD)

        keys = project(w_key)
        values = project(w_value)
        state = jnp.einsum("jhd,jhe->hde", keys, values, preferred_element_type=F32)
        query = project(w_query)
        history = jnp.zeros_like(state)
        total = state
        for bit in seq_bits:
            other = swap(total.astype(BF16), "seq", bit).astype(F32)
            history = history + jnp.where((me_seq & bit) != 0, other, 0.0)
            total = total + other
            if bit in last:
                wide_far, total = after(wide_far, total)
        history = history.astype(BF16)
        (tall_give, history) = after({pair: down_give}, history)
        wide_got, history = after(wide_got, history)
        tall_got = {pair: swap(tall_give[pair], "seq", pair)}
        for bit in first:
            wide_got.update(hops(wide_got, [bit]))
        near = {**wide_near, **hops({r: v for r, v in wide_far.items() if r}, last)}
        wide = {**wide_far, **near}
        scores = jnp.einsum("ihd,jhd->hij", query, keys, preferred_element_type=F32)
        causal = jnp.arange(length)[:, None] >= jnp.arange(length)[None, :]
        scores = jnp.where(causal[None], scores, 0.0).astype(BF16)
        inside = jnp.einsum("hij,jhd->ihd", scores, values, preferred_element_type=F32)
        wide_got.update(hops(wide_got, last))
        wide.update(wide_got)
        carried = jnp.einsum(
            "ihd,hde->ihe", query, history, preferred_element_type=F32
        )
        mixed = inside + carried
        scale = lax.rsqrt(jnp.mean(mixed * mixed, axis=-1, keepdims=True) + 1e-06)
        normed = (mixed * scale * head_gain.reshape(heads, HD)).astype(BF16)
        normed = normed.reshape(length, heads * HD)
        resid = tokens.astype(F32) + to_features(normed, w_out)
        gain = lax.dynamic_slice_in_dim(norm_gain, me_tp * width, width, 0)
        own_in = (resid * gain).astype(BF16)
        pair_in = swap(own_in, "seq", pair)
        own_pieces = gather_tp(own_in)
        pair_pieces = gather_tp(pair_in)
        tall_far, own_in = after({r: v for r, v in tall_far.items() if r}, own_in)
        tall_got, own_in = after(tall_got, own_in)
        tall = {**tall_own, **tall_near, **tall_far, **hops(tall_far, last)}
        for bit in first:
            tall_got.update(hops(tall_got, [bit]))
        tall_got.update(hops(tall_got, last))
        tall.update(tall_got)
        squares = jnp.sum(resid * resid, axis=-1)
        for bit in tp_bits:
            squares = squares + swap(squares, "tp", bit)
        pair_squares = swap(squares, "seq", pair)
        wide_whole = assemble(wide, 0)
        gate_whole, up_whole = wide_whole[:, :half], wide_whole[:, half:]
        down_whole = assemble(tall, 1)

        def feed(pieces, total):
            factor = lax.rsqrt(total / model + 1e-05)[:, None]
            ffn_in = side_by_side(pieces)
            gate = matmul(ffn_in, gate_whole) * factor
            upward = matmul(ffn_in, up_whole) * factor
            hidden = (jax.nn.silu(gate) * upward).astype(BF16)
            return to_features(hidden, down_whole)

        pair_out = feed(pair_pieces, pair_squares)
        own_out = feed(own_pieces, squares)
        back = swap(pair_out.astype(BF16), "seq", pair)
        return (resid + own_out + back.astype(F32)).astype(BF16)

    return body


def solution(mesh):
    body = make_body(mesh.shape["seq"], mesh.shape["tp"])

    return jax.shard_map(
        body,
        mesh=mesh,
        in_specs=(
            P("seq", "tp"),
            P(None, "tp"),
            P(None, "tp"),
            P(None, "tp"),
            P("tp"),
            P("tp", None),
            P(),
            P("seq", "tp"),
            P("seq", "tp"),
            P("tp", "seq"),
        ),
        out_specs=P("seq", "tp"),
        check_vma=False,
    )
```

```python
import jax
import jax.numpy as jnp
from jax import lax
from jax.experimental.layout import Layout, with_layout_constraint
from jax.sharding import PartitionSpec as P

HD = 128
F32 = jnp.float32
BF16 = jnp.bfloat16


def make_body(n_seq, n_tp):
    pair = n_seq // 2
    seq_bits = [1 << b for b in range(n_seq.bit_length() - 1)]
    tp_bits = [1 << b for b in range(n_tp.bit_length() - 1)]
    spread_bits = [b for b in reversed(seq_bits) if b != pair]

    def swap(value, axis, bit):
        size = n_seq if axis == "seq" else n_tp
        return lax.ppermute(value, axis, [(i, i ^ bit) for i in range(size)])

    def spread(held, axis, bits):
        held = dict(held)
        for bit in bits:
            for r in list(held):
                held[r ^ bit] = swap(held[r], axis, bit)
        return held

    def gather_tp(value):
        return spread({0: value}, "tp", list(reversed(tp_bits)))

    def scatter_tp(terms):
        terms = dict(terms)
        for bit in tp_bits:
            for r in [r for r in terms if r & bit]:
                moved = swap(terms.pop(r).astype(BF16), "tp", bit)
                terms[r ^ bit] = terms[r ^ bit] + moved.astype(F32)
        return terms[0]

    def body(tokens, w_query, w_key, w_value, head_gain, w_out, norm_gain, w_gate, w_up, w_down):
        length, width = tokens.shape
        heads = w_query.shape[1] // HD
        model = norm_gain.shape[0]
        me_seq = lax.axis_index("seq")
        me_tp = lax.axis_index("tp")
        part = ((me_seq & pair) != 0).astype(jnp.int32)
        half = w_gate.shape[1] // 2
        rows = w_gate.shape[0]

        def halves(weight, dim):
            keep = lax.dynamic_slice_in_dim(weight, part * half, half, dim)
            give = lax.dynamic_slice_in_dim(weight, (1 - part) * half, half, dim)
            return keep, give

        def assemble(pieces, dim):
            shape = list(pieces[0].shape)
            shape[dim] = n_seq * rows
            out = jnp.zeros(shape, BF16)
            for r, piece in pieces.items():
                out = lax.dynamic_update_slice_in_dim(out, piece, (me_seq ^ r) * rows, dim)
            return out

        def after(values, anchor):
            keys_of = list(values)
            out = lax.optimization_barrier(tuple(values[k] for k in keys_of) + (anchor,))
            return dict(zip(keys_of, out[:-1])), out[-1]

        def hops(pieces, bits):
            return {r ^ bit: swap(v, "seq", bit) for bit in bits for r, v in pieces.items()}

        def matmul(a, b):
            return jnp.dot(a, b, preferred_element_type=F32)

        def side_by_side(pieces):
            out = jnp.zeros((length, model), BF16)
            for r in sorted(pieces):
                out = lax.dynamic_update_slice_in_dim(out, pieces[r], (me_tp ^ r) * width, 1)
            return out

        def to_features(value, weight):
            terms = {}
            for r in reversed(range(n_tp)):
                block = lax.dynamic_slice_in_dim(weight, (me_tp ^ r) * width, width, 1)
                terms[r] = matmul(value, block)
            return scatter_tp(terms)

        first, last = spread_bits[:-1], spread_bits[-1:]
        gate_keep, gate_give = halves(w_gate, 1)
        up_keep, up_give = halves(w_up, 1)
        down_keep, down_give = halves(w_down, 0)
        wide_own = {0: jnp.concatenate([gate_keep, up_keep], axis=1)}
        wide_give = jnp.concatenate([gate_give, up_give], axis=1)
        tall_own = {0: down_keep}

        token_pieces = gather_tp(tokens)
        features = with_layout_constraint(side_by_side(token_pieces), Layout((0, 1)))
        wide_got = {pair: swap(wide_give, "seq", pair)}
        wide_far = dict(wide_own)
        for bit in first:
            wide_far.update(hops(wide_far, [bit]))
        wide_near = hops(wide_own, last)
        tall_far = dict(tall_own)
        for bit in first:
            tall_far.update(hops(tall_far, [bit]))
        tall_near = hops(tall_own, last)

        def project(weight):
            return matmul(features, weight).astype(BF16).reshape(length, heads, HD)

        keys = project(w_key)
        values = project(w_value)
        state = jnp.einsum("jhd,jhe->hde", keys, values, preferred_element_type=F32)
        query = project(w_query)
        history = jnp.zeros_like(state)
        total = state
        for bit in seq_bits:
            other = swap(total.astype(BF16), "seq", bit).astype(F32)
            history = history + jnp.where((me_seq & bit) != 0, other, 0.0)
            total = total + other
            if bit in last:
                wide_far, total = after(wide_far, total)
        history = history.astype(BF16)
        (tall_give, history) = after({pair: down_give}, history)
        wide_got, history = after(wide_got, history)
        tall_got = {pair: swap(tall_give[pair], "seq", pair)}
        got_near = hops({pair: wide_got[pair]}, last)
        for bit in first:
            wide_got.update(hops(wide_got, [bit]))
        far_near = hops({r: v for r, v in wide_far.items() if r}, last)
        near = {**wide_near, **far_near, **got_near}
        wide = {**wide_far, **near}
        scores = jnp.einsum("ihd,jhd->hij", query, keys, preferred_element_type=F32)
        causal = jnp.arange(length)[:, None] >= jnp.arange(length)[None, :]
        scores = jnp.where(causal[None], scores, 0.0).astype(BF16)
        inside = jnp.einsum("hij,jhd->ihd", scores, values, preferred_element_type=F32)
        wide.update(wide_got)
        wide.update(hops({r: v for r, v in wide_got.items() if r != pair}, last))
        carried = jnp.einsum(
            "ihd,hde->ihe", query, history, preferred_element_type=F32
        )
        mixed = inside + carried
        scale = lax.rsqrt(jnp.mean(mixed * mixed, axis=-1, keepdims=True) + 1e-06)
        normed = (mixed * scale * head_gain.reshape(heads, HD)).astype(BF16)
        normed = normed.reshape(length, heads * HD)
        attended = to_features(normed, w_out)
        resid = tokens.astype(F32) + attended
        gain = lax.dynamic_slice_in_dim(norm_gain, me_tp * width, width, 0)
        own_in = (resid * gain).astype(BF16)
        pair_in = swap(own_in, "seq", pair)
        own_pieces = gather_tp(own_in)
        pair_pieces = gather_tp(pair_in)
        tall_far, own_in = after({r: v for r, v in tall_far.items() if r}, own_in)
        tall_got, own_in = after(tall_got, own_in)
        tall = {**tall_own, **tall_near, **tall_far, **hops(tall_far, last)}
        for bit in first:
            tall_got.update(hops(tall_got, [bit]))
        tall_got.update(hops(tall_got, last))
        tall.update(tall_got)
        squares = jnp.sum(resid * resid, axis=-1)
        for bit in tp_bits:
            squares = squares + swap(squares, "tp", bit)
        pair_squares = swap(squares, "seq", pair)
        wide_whole = assemble(wide, 0)
        gate_whole, up_whole = wide_whole[:, :half], wide_whole[:, half:]
        down_whole = assemble(tall, 1)

        def feed(pieces, total):
            factor = lax.rsqrt(total / model + 1e-05)[:, None]
            ffn_in = side_by_side(pieces)
            gate = matmul(ffn_in, gate_whole)
            upward = matmul(ffn_in, up_whole) * factor
            gate = gate * factor
            hidden = (jax.nn.silu(gate) * upward).astype(BF16)
            return to_features(hidden, down_whole)

        pair_out = feed(pair_pieces, pair_squares)
        own_out = feed(own_pieces, squares)
        back = swap(pair_out.astype(BF16), "seq", pair)
        return (resid + own_out + back.astype(F32)).astype(BF16)

    return body


def solution(mesh):
    body = make_body(mesh.shape["seq"], mesh.shape["tp"])

    return jax.shard_map(
        body,
        mesh=mesh,
        in_specs=(
            P("seq", "tp"),
            P(None, "tp"),
            P(None, "tp"),
            P(None, "tp"),
            P("tp"),
            P("tp", None),
            P(),
            P("seq", "tp"),
            P("seq", "tp"),
            P("tp", "seq"),
        ),
        out_specs=P("seq", "tp"),
        check_vma=False,
    )
```
